256 devices in a mesh: view: 8 (over z_hi, core), gauss: 32 (over z_lo, x, y).
Axes of the slice: x: 4, y: 4, z: 8 (z_hi: 4, z_lo: 2; z = z_hi * 2 + z_lo), core: 2. Of those that a mesh axis runs over, the one named last changes fastest.
Arguments:
- entry_grads: bfloat16 [8, 59, 655360], P('view', None, 'gauss'), may hold values from -4 to 4
- vis_ids: int32 [8, 655360], P('view', 'gauss'), may hold values from 0 to 20479
- feats: bfloat16 [256, 32, 20480], P(None, 'gauss', 'view'), may hold values from -6 to 6
- code_tab: float32 [256, 8], replicated, may hold values from -4 to 4
- subj_ids: int32 [32, 20480], P('gauss', 'view'), may hold values from 0 to 7
- bone_ids: int32 [4, 32, 20480], P(None, 'gauss', 'view'), may hold values from 0 to 23
- skin_w: float32 [4, 32, 20480], P(None, 'gauss', 'view'), may hold values from 0.05 to 0.5
- canon_pos: float32 [3, 32, 20480], P(None, 'gauss', 'view'), may hold values from -5 to 5
- bone_tf: float32 [12, 192], replicated, may hold values from -4 to 4
- w_first: bfloat16 [256, 256], replicated, may hold values from -0.375 to 0.375
- w_second: bfloat16 [256, 256], replicated, may hold values from -0.375 to 0.375
- w_third: bfloat16 [256, 256], replicated, may hold values from -0.375 to 0.375
- biases: float32 [3, 256], replicated, may hold values from -3 to 3
- w_head: bfloat16 [3, 256], replicated, may hold values from -0.375 to 0.375
Outputs:
- attr_grads: float32 [59, 32, 20480], P(None, 'gauss', 'view')
- feat_grads: bfloat16 [256, 32, 20480], P(None, 'gauss', 'view')
- skin_grads: float32 [4, 32, 20480], P(None, 'gauss', 'view')
- first_grad: float32 [256, 256], replicated
- second_grad: float32 [256, 256], replicated
- third_grad: float32 [256, 256], replicated
- bias_grads: float32 [3, 256], replicated
- head_grad: float32 [3, 256], replicated
- code_grad: float32 [256, 8], replicated
- bone_grad: float32 [12, 192], replicated
The draws below stay inside these ranges and needn't reach their ends.
All inputs are finite; a program needn't handle non-finite values.
Results may differ from the reference program's by a relative error of at most 0.024.
Values may be sent and summed in bfloat16 or wider, within the bound.
A program may use at most 128 MiB of HBM per device.

```python
import math
import jax
import jax.numpy as jnp
from jax import lax

ATTRS = 59
WIDTH = 256
BONES = 24
INFLUENCE = 4
SUBJECTS = 8
VIEWS = 8
SHARDS = 32
GAUSS_PER_PART = 20480
ENTRIES = 655360
GAUSSIANS = 655360


def plant(drawn, rng, least, largest):
    dims = drawn.shape
    spot = [jax.random.randint(jax.random.fold_in(rng, axis), (), 0, dims[axis]) for axis in range(len(dims))]
    drawn = drawn.at[tuple(spot)].set(least)
    longest = dims.index(max(dims))
    spot[longest] = (spot[longest] + 1) % dims[longest]
    return drawn.at[tuple(spot)].set(largest)


def steps_of(key, shape, pieces, low, high):
    level = 1.0
    for dim, blocks in pieces:
        steps = jax.random.uniform(jax.random.fold_in(jax.random.fold_in(key, 6), dim), (blocks,), jnp.float32, low / len(pieces), high / len(pieces))
        level = level * jnp.repeat(jnp.exp(steps), shape[dim] // blocks).reshape((-1,) + (1,) * (len(shape) - 1 - dim))
    return level


def bell_draw(stream_key, shape, deviation, reach, split=(), held_as=jnp.bfloat16):
    loudness = steps_of(stream_key, shape, split, -0.22, 0.18) if split else 1.0
    result = jax.random.normal(stream_key, shape, jnp.float32) * deviation * loudness
    return jnp.minimum(jnp.maximum(result, -reach), reach).astype(held_as)


def setup_inputs(seed: int = 0) -> dict:
    arg_keys = jax.random.split(jax.random.key(seed), 15)
    entry_grads = bell_draw(arg_keys[0], (VIEWS, ATTRS, ENTRIES), 0.5, 4.0, ((0, 8), (2, 32)))
    vis_ids = plant(jax.random.randint(arg_keys[1], (VIEWS, ENTRIES), 0, GAUSS_PER_PART), jax.random.fold_in(arg_keys[1], 1), 0, GAUSS_PER_PART - 1).astype(jnp.int32)
    feats = bell_draw(arg_keys[2], (WIDTH, SHARDS, GAUSS_PER_PART), 1.0, 6.0, ((1, 32), (2, 8)))
    code_tab = bell_draw(arg_keys[3], (WIDTH, SUBJECTS), 0.5, 4.0, (), jnp.float32)
    subj_ids = plant(jax.random.randint(arg_keys[4], (SHARDS, GAUSS_PER_PART), 0, SUBJECTS), jax.random.fold_in(arg_keys[4], 1), 0, SUBJECTS - 1).astype(jnp.int32)
    bone_ids = plant(jax.random.randint(arg_keys[5], (INFLUENCE, SHARDS, GAUSS_PER_PART), 0, BONES), jax.random.fold_in(arg_keys[5], 1), 0, BONES - 1).astype(jnp.int32)
    skin_w = jnp.clip(0.05 + 0.45 * jax.random.uniform(arg_keys[6], (INFLUENCE, SHARDS, GAUSS_PER_PART), jnp.float32) ** steps_of(arg_keys[6], (INFLUENCE, SHARDS, GAUSS_PER_PART), ((1, 32), (2, 8)), -0.2, 0.2), 0.05, 0.5)
    canon_pos = bell_draw(arg_keys[7], (3, SHARDS, GAUSS_PER_PART), 1.0, 5.0, ((1, 32), (2, 8)), jnp.float32)
    bone_tf = bell_draw(arg_keys[8], (12, SUBJECTS * BONES), 0.6, 4.0, (), jnp.float32)
    w_first = bell_draw(arg_keys[9], (WIDTH, WIDTH), WIDTH ** -0.5, 0.375)
    w_second = bell_draw(arg_keys[10], (WIDTH, WIDTH), WIDTH ** -0.5, 0.375)
    w_third = bell_draw(arg_keys[11], (WIDTH, WIDTH), WIDTH ** -0.5, 0.375)
    biases = bell_draw(arg_keys[12], (3, WIDTH), 0.5, 3.0, (), jnp.float32)
    w_head = bell_draw(arg_keys[13], (3, WIDTH), WIDTH ** -0.5, 0.375)
    return dict(entry_grads=entry_grads, vis_ids=vis_ids, feats=feats, code_tab=code_tab, subj_ids=subj_ids, bone_ids=bone_ids, skin_w=skin_w, canon_pos=canon_pos, bone_tf=bone_tf, w_first=w_first, w_second=w_second, w_third=w_third, biases=biases, w_head=w_head)


def dsilu(value):
    sig = jax.nn.sigmoid(value)
    return sig * (1.0 + value * (1.0 - sig))

def reference(entry_grads, vis_ids, feats, code_tab, subj_ids, bone_ids, skin_w, canon_pos, bone_tf, w_first, w_second, w_third, biases, w_head):
    table_cols = SUBJECTS * BONES

    def one_shard(carry, block_index):
        first_col = (block_index * GAUSS_PER_PART).astype(jnp.int32)
        values = lax.dynamic_slice_in_dim(entry_grads, first_col, GAUSS_PER_PART, 2)
        indices = lax.dynamic_slice_in_dim(vis_ids, first_col, GAUSS_PER_PART, 1)
        summed = jnp.zeros((ATTRS, GAUSS_PER_PART), jnp.float32)
        for viewer in range(VIEWS):
            partial_value = jnp.zeros((ATTRS, GAUSS_PER_PART), jnp.float32).at[:, indices[viewer]].add(values[viewer].astype(jnp.float32))
            rounded = lax.optimization_barrier(partial_value.astype(jnp.bfloat16))
            summed = summed + rounded.astype(jnp.float32)
        features = lax.dynamic_index_in_dim(feats, block_index, 1, keepdims=False)
        subject = lax.dynamic_index_in_dim(subj_ids, block_index, 0, keepdims=False)
        chosen = lax.dynamic_index_in_dim(bone_ids, block_index, 1, keepdims=False)
        skinning_weight = lax.dynamic_index_in_dim(skin_w, block_index, 1, keepdims=False)
        canon = lax.dynamic_index_in_dim(canon_pos, block_index, 1, keepdims=False)
        inputs = (features.astype(jnp.float32) + jnp.take(code_tab, subject, axis=1)).astype(jnp.bfloat16)
        pre_one = jnp.dot(w_first, inputs, preferred_element_type=jnp.float32) + biases[0][:, None]
        act_one = jax.nn.silu(pre_one).astype(jnp.bfloat16)
        pre_two = jnp.dot(w_second, act_one, preferred_element_type=jnp.float32) + biases[1][:, None]
        act_two = jax.nn.silu(pre_two).astype(jnp.bfloat16)
        pre_three = jnp.dot(w_third, act_two, preferred_element_type=jnp.float32) + biases[2][:, None]
        act_three = jax.nn.silu(pre_three).astype(jnp.bfloat16)
        shifted_point = canon + jnp.dot(w_head, act_three, preferred_element_type=jnp.float32)
        homogeneous_point = jnp.concatenate([shifted_point, jnp.ones((1, GAUSS_PER_PART), jnp.float32)], axis=0)
        position_gradient = summed[:3]
        shift_acc = jnp.zeros((3, GAUSS_PER_PART), jnp.float32)
        bone_acc = jnp.zeros((12, table_cols), jnp.float32)
        skins = []
        for member_flag in range(INFLUENCE):
            column = (subject * BONES + chosen[member_flag]).astype(jnp.int32)
            blend_matrix = jnp.take(bone_tf, column, axis=1).reshape(3, 4, GAUSS_PER_PART)
            posed_point = lax.optimization_barrier(jnp.sum(blend_matrix * homogeneous_point[None], axis=1))
            skins.append(lax.optimization_barrier(jnp.sum(position_gradient * posed_point, axis=0)))
            shift_acc = shift_acc + skinning_weight[member_flag] * lax.optimization_barrier(jnp.sum(blend_matrix[:, :3] * position_gradient[:, None], axis=0))
            contribution = ((skinning_weight[member_flag] * position_gradient)[:, None] * homogeneous_point[None]).reshape(12, GAUSS_PER_PART)
            bone_acc = bone_acc + jax.ops.segment_sum(contribution.T, column, num_segments=table_cols).T
        shift_grad = shift_acc.astype(jnp.bfloat16)
        head = jnp.dot(shift_grad, act_three.T, preferred_element_type=jnp.float32)
        back_three = (jnp.dot(w_head.T, shift_grad, preferred_element_type=jnp.float32) * dsilu(pre_three)).astype(jnp.bfloat16)
        third = jnp.dot(back_three, act_two.T, preferred_element_type=jnp.float32)
        back_two = (jnp.dot(w_third.T, back_three, preferred_element_type=jnp.float32) * dsilu(pre_two)).astype(jnp.bfloat16)
        second = jnp.dot(back_two, act_one.T, preferred_element_type=jnp.float32)
        back_one = (jnp.dot(w_second.T, back_two, preferred_element_type=jnp.float32) * dsilu(pre_one)).astype(jnp.bfloat16)
        first = jnp.dot(back_one, inputs.T, preferred_element_type=jnp.float32)
        bias_rows = jnp.stack([lax.optimization_barrier(jnp.sum(back_one.astype(jnp.float32), axis=1)), lax.optimization_barrier(jnp.sum(back_two.astype(jnp.float32), axis=1)), lax.optimization_barrier(jnp.sum(back_three.astype(jnp.float32), axis=1))])
        input_grad = jnp.dot(w_first.T, back_one, preferred_element_type=jnp.float32)
        code = jax.ops.segment_sum(input_grad.T, subject.astype(jnp.int32), num_segments=SUBJECTS).T
        sums = (first, second, third, bias_rows, head, code, bone_acc)
        carry = tuple((old + new for old, new in zip(carry, sums)))
        return (carry, (summed, input_grad.astype(jnp.bfloat16), jnp.stack(skins)))
    start = (jnp.zeros((WIDTH, WIDTH), jnp.float32), jnp.zeros((WIDTH, WIDTH), jnp.float32), jnp.zeros((WIDTH, WIDTH), jnp.float32), jnp.zeros((3, WIDTH), jnp.float32), jnp.zeros((3, WIDTH), jnp.float32), jnp.zeros((WIDTH, SUBJECTS), jnp.float32), jnp.zeros((12, table_cols), jnp.float32))
    totals, stacked = lax.scan(one_shard, start, jnp.arange(SHARDS, dtype=jnp.int32))
    factor = 1.0 / math.sqrt(GAUSSIANS)
    first, second, third, bias_rows, head, code, bone_acc = [factor * value for value in totals]
    attr_grads = jnp.transpose(stacked[0], (1, 0, 2))
    feat_grads = jnp.transpose(stacked[1], (1, 0, 2))
    skin_grads = jnp.transpose(stacked[2], (1, 0, 2))
    return (attr_grads, feat_grads, skin_grads, first, second, third, bias_rows, head, code, bone_acc)
```

```python
import functools
import math

import jax
import jax.numpy as jnp
from jax import lax
from jax.experimental import pallas as pl
from jax.experimental.pallas import tpu as pltpu
from jax.sharding import PartitionSpec as P

HIGH = lax.Precision.HIGHEST


def dsilu(value):
    sig = jax.nn.sigmoid(value)
    return sig * (1.0 + value * (1.0 - sig))


def over_rows(left, right):
    return lax.dot_general(
        left, right, (((1,), (1,)), ((), ())), preferred_element_type=jnp.float32
    )


def over_first(left, right):
    return lax.dot_general(
        left, right, (((0,), (0,)), ((), ())), preferred_element_type=jnp.float32
    )


ENTRY_COUNT, ATTRS, GAUSS = 20480, 59, 20480
HALF = GAUSS // 2
BLOCK = 128
def scatter_kernel(K, UF, rows_ref, ids_ref, grads_ref, out_ref, vals_a, vals_b, *accs):
    def zero(i, c):
        for a in accs:
            a[pl.ds(pl.multiple_of(i * 128, 128), 128), :] = jnp.zeros((128, 128), jnp.float32)
        return c
    lax.fori_loop(0, HALF // 128, zero, 0)
    def tr(off, vals):
        for b in range(BLOCK // 128):
            o = pl.multiple_of(off + b * 128, 128)
            x = grads_ref[0, :, pl.ds(o, 128)].astype(jnp.float32)
            x = jnp.concatenate([x, jnp.zeros((64 - ATTRS, 128), jnp.float32)], axis=0)
            hi = ids_ref[:, pl.ds(o, 128)] >= HALF
            m = jnp.concatenate([jnp.where(hi, 0.0, x), jnp.where(hi, x, 0.0)], axis=0)
            vals[b * 128:(b + 1) * 128, :] = m.T
    def rmw(off, vals):
        for j in range(BLOCK // K):
            r = [rows_ref[off + j * K + k] for k in range(K)]
            new = [accs[k][pl.ds(r[k], 1), :] + vals[j * K + k:j * K + k + 1, :] for k in range(K)]
            for k in range(K):
                accs[k][pl.ds(r[k], 1), :] = new[k]
    tr(0, vals_a)
    def step(i, c):
        off = pl.multiple_of(i * (2 * BLOCK), 2 * BLOCK)
        tr(off + BLOCK, vals_b)
        rmw(off, vals_a)
        tr(jnp.minimum(off + 2 * BLOCK, ENTRY_COUNT - BLOCK), vals_a)
        rmw(off + BLOCK, vals_b)
        return c
    lax.fori_loop(0, ENTRY_COUNT // (2 * BLOCK), step, 0)
    def fin(i, c):
        for u in range(UF):
            off = pl.multiple_of(i * (128 * UF) + u * 128, 128)
            s = accs[0][pl.ds(off, 128), :]
            for a in accs[1:]:
                s = s + a[pl.ds(off, 128), :]
            t = s.T.astype(jnp.bfloat16)
            out_ref[:, pl.ds(off, 128)] = t[:ATTRS]
            out_ref[:, pl.ds(pl.multiple_of(HALF + off, 128), 128)] = t[64:64 + ATTRS]
        return c
    lax.fori_loop(0, HALF // (128 * UF), fin, 0)

def scatter(grads, ids, K=8, UF=4):
    ids1 = ids.reshape(-1)
    rows = jnp.where(ids1 >= HALF, ids1 - HALF, ids1)
    return pl.pallas_call(
        functools.partial(scatter_kernel, K, UF),
        out_shape=jax.ShapeDtypeStruct((ATTRS, GAUSS), jnp.bfloat16),
        in_specs=[pl.BlockSpec(memory_space=pltpu.SMEM), pl.BlockSpec(memory_space=pltpu.VMEM), pl.BlockSpec(memory_space=pltpu.VMEM)],
        out_specs=pl.BlockSpec(memory_space=pltpu.VMEM),
        scratch_shapes=[pltpu.VMEM((BLOCK, 128), jnp.float32)] * 2 + [pltpu.VMEM((HALF, 128), jnp.float32)] * K,
        compiler_params=pltpu.CompilerParams(vmem_limit_bytes=62 * 1024 * 1024),
    )(rows, ids.reshape(1, -1), grads)


MESH = pl.DeviceIdType.MESH
PIECE, PLANE, DEPTH = 56, 16, 8


def place():
    view, gauss = lax.axis_index("view"), lax.axis_index("gauss")
    return view // 2, lax.rem(view, 2), gauss // PLANE, lax.rem(gauss, PLANE)


def plane_peer(step):
    high, core, low, spot = place()
    return (high * 2 + core, low * PLANE + lax.rem(spot + step, PLANE))


def depth_peer(step):
    high, core, low, spot = place()
    level = lax.rem(high * 2 + low + step, DEPTH)
    return ((level // 2) * 2 + core, lax.rem(level, 2) * PLANE + spot)


def core_peer():
    high, core, low, spot = place()
    return (high * 2 + 1 - core, low * PLANE + spot)


def greet(barrier, peers, count):
    def one(step, carry):
        pl.semaphore_signal(barrier, inc=1, device_id=peers(step), device_id_type=MESH)
        return carry

    lax.fori_loop(1, count, one, 0)


def remote(src, dst, sems, step, peer):
    return pltpu.make_async_remote_copy(
        src_ref=src,
        dst_ref=dst,
        send_sem=sems.at[0, step],
        recv_sem=sems.at[1, step],
        device_id=peer,
        device_id_type=MESH,
    )


def each(count, action):
    def one(step, carry):
        action(step)
        return carry

    lax.fori_loop(1, count, one, 0)


def reduce_all(pay, out, near, plane, depth, sems_near, sems_plane, sems_depth, sems_back):
    high, core, low, spot = place()
    level = high * 2 + low
    swap = remote(pay.at[1 - core], near, sems_near, 0, core_peer())
    swap.start()
    swap.wait()
    near[...] = near[...] + pay[core]

    def plane_copy(step):
        return remote(near.at[lax.rem(spot + step, PLANE)], plane.at[spot], sems_plane, step, plane_peer(step))

    each(PLANE, lambda step: plane_copy(step).start())
    plane[spot] = near[spot]
    each(PLANE, lambda step: plane_copy(step).wait())
    total = plane[0]
    for index in range(1, PLANE):
        total = total + plane[index]
    depth[level] = total

    def depth_copy(step):
        return remote(depth.at[level], depth.at[level], sems_depth, step, depth_peer(step))

    each(DEPTH, lambda step: depth_copy(step).start())
    each(DEPTH, lambda step: depth_copy(step).wait())
    total = depth[0]
    for index in range(1, DEPTH):
        total = total + depth[index]
    out[core, spot] = total

    def back_copy(step):
        return remote(out.at[core, spot], out.at[core, spot], sems_back, step, plane_peer(step))

    each(PLANE, lambda step: back_copy(step).start())
    each(PLANE, lambda step: back_copy(step).wait())
    last = remote(out.at[core], out.at[core], sems_near, 1, core_peer())
    last.start()
    last.wait()


def reduce_kernel(pay, out, near, plane, depth, sems_near, sems_plane, sems_depth, sems_back):
    barrier = pltpu.get_barrier_semaphore()
    greet(barrier, plane_peer, PLANE)
    greet(barrier, depth_peer, DEPTH)
    pl.semaphore_signal(barrier, inc=1, device_id=core_peer(), device_id_type=MESH)
    pl.semaphore_wait(barrier, PLANE - 1 + DEPTH - 1 + 1)
    reduce_all(pay, out, near, plane, depth, sems_near, sems_plane, sems_depth, sems_back)


REDUCE_SCRATCH = [
    pltpu.VMEM((PLANE, PIECE, 128), jnp.float32),
    pltpu.VMEM((PLANE, PIECE, 128), jnp.float32),
    pltpu.VMEM((DEPTH, PIECE, 128), jnp.float32),
    pltpu.SemaphoreType.DMA((2, 2)),
    pltpu.SemaphoreType.DMA((2, PLANE)),
    pltpu.SemaphoreType.DMA((2, DEPTH)),
    pltpu.SemaphoreType.DMA((2, PLANE)),
]


def reduce_call(pay):
    return pl.pallas_call(
        reduce_kernel,
        out_shape=jax.ShapeDtypeStruct((2, PLANE, PIECE, 128), jnp.float32),
        in_specs=[pl.BlockSpec(memory_space=pltpu.VMEM)],
        out_specs=pl.BlockSpec(memory_space=pltpu.VMEM),
        scratch_shapes=REDUCE_SCRATCH,
        compiler_params=pltpu.CompilerParams(collective_id=0, has_side_effects=True),
        name="reduce_all",
    )(pay)


def pack(first, second, third, small):
    rows = jnp.concatenate([first, second, third, small], axis=0)
    return jnp.stack([rows[:, :128], rows[:, 128:]]).reshape(2, PLANE, PIECE, 128)


def body(
    entry_grads,
    vis_ids,
    feats,
    code_tab,
    subj_ids,
    bone_ids,
    skin_w,
    canon_pos,
    bone_tf,
    w_first,
    w_second,
    w_third,
    biases,
    w_head,
):
    member_count = feats.shape[2]
    viewers = lax.axis_size("view")
    factor = 1.0 / math.sqrt(member_count * viewers * lax.axis_size("gauss"))
    partial_value = scatter(entry_grads, vis_ids)
    summed = lax.psum_scatter(partial_value, "view", scatter_dimension=1, tiled=True).astype(
        jnp.float32
    )
    position_gradient = summed[:3]
    subjects = code_tab.shape[1]
    table_cols = bone_tf.shape[1]
    per_subject = table_cols // subjects
    subject = subj_ids[0]
    subj_hot = (subject[None, :] == jnp.arange(subjects, dtype=jnp.int32)[:, None]).astype(
        jnp.float32
    )
    code_sel = jnp.dot(code_tab, subj_hot, precision=HIGH)
    inputs = (feats[:, 0].astype(jnp.float32) + code_sel).astype(jnp.bfloat16)
    pre_one = jnp.dot(w_first, inputs, preferred_element_type=jnp.float32) + biases[0][:, None]
    act_one = jax.nn.silu(pre_one).astype(jnp.bfloat16)
    pre_two = jnp.dot(w_second, act_one, preferred_element_type=jnp.float32) + biases[1][:, None]
    act_two = jax.nn.silu(pre_two).astype(jnp.bfloat16)
    pre_three = jnp.dot(w_third, act_two, preferred_element_type=jnp.float32) + biases[2][:, None]
    act_three = jax.nn.silu(pre_three).astype(jnp.bfloat16)
    shifted_point = canon_pos[:, 0] + jnp.dot(w_head, act_three, preferred_element_type=jnp.float32)
    homogeneous_point = jnp.concatenate(
        [shifted_point, jnp.ones((1, member_count), jnp.float32)], axis=0
    )
    table_index = jnp.arange(table_cols, dtype=jnp.int32)[:, None]
    shift_acc = jnp.zeros((3, member_count), jnp.float32)
    bone_acc = jnp.zeros((12, table_cols), jnp.float32)
    skins = []
    for member_flag in range(bone_ids.shape[0]):
        column = subject * per_subject + bone_ids[member_flag, 0]
        onehot = (column[None, :] == table_index).astype(jnp.float32)
        blend_matrix = jnp.dot(bone_tf, onehot, precision=HIGH).reshape(3, 4, member_count)
        skinning_weight = skin_w[member_flag, 0]
        posed_point = jnp.sum(blend_matrix * homogeneous_point[None], axis=1)
        skins.append(jnp.sum(position_gradient * posed_point, axis=0))
        shift_acc = shift_acc + skinning_weight * jnp.sum(
            blend_matrix[:, :3] * position_gradient[:, None], axis=0
        )
        contribution = (
            (skinning_weight * position_gradient)[:, None] * homogeneous_point[None]
        ).reshape(12, member_count)
        bone_acc = bone_acc + lax.dot_general(
            contribution, onehot, (((1,), (1,)), ((), ())), precision=HIGH
        )
    shift_grad = shift_acc.astype(jnp.bfloat16)
    head = over_rows(shift_grad, act_three)
    back_three = (over_first(w_head, shift_grad) * dsilu(pre_three)).astype(jnp.bfloat16)
    third = over_rows(back_three, act_two)
    bias_three = jnp.sum(back_three, axis=1, dtype=jnp.float32)
    bone_total = bone_acc
    back_two = (over_first(w_third, back_three) * dsilu(pre_two)).astype(jnp.bfloat16)
    second = over_rows(back_two, act_one)
    bias_two = jnp.sum(back_two, axis=1, dtype=jnp.float32)
    back_one = (over_first(w_second, back_two) * dsilu(pre_one)).astype(jnp.bfloat16)
    first = over_rows(back_one, inputs)
    bias_one = jnp.sum(back_one, axis=1, dtype=jnp.float32)
    input_grad = over_first(w_first, back_one)
    code = lax.dot_general(subj_hot, input_grad, (((1,), (1,)), ((), ())), precision=HIGH)
    small = jnp.concatenate(
        [
            head,
            bias_one[None],
            bias_two[None],
            bias_three[None],
            code,
            jnp.pad(bone_total, ((0, 128 - 26), (0, 256 - table_cols))),
        ],
        axis=0,
    )
    whole = factor * reduce_call(pack(first, second, third, small)).reshape(2, 896, 128)
    whole = jnp.concatenate([whole[0], whole[1]], axis=1)
    first, second, third = whole[:256], whole[256:512], whole[512:768]
    head, bias_rows, code = whole[768:771], whole[771:774], whole[774:782].T
    bone_total = whole[782:794, :table_cols]
    return (
        summed[:, None, :],
        input_grad.astype(jnp.bfloat16)[:, None, :],
        jnp.stack(skins)[:, None, :],
        first,
        second,
        third,
        bias_rows,
        head,
        code,
        bone_total,
    )


def solution(mesh):
    placed = (
        P("view", None, "gauss"),
        P("view", "gauss"),
        P(None, "gauss", "view"),
        P(),
        P("gauss", "view"),
        P(None, "gauss", "view"),
        P(None, "gauss", "view"),
        P(None, "gauss", "view"),
        P(),
        P(),
        P(),
        P(),
        P(),
        P(),
    )
    return jax.shard_map(
        body,
        mesh=mesh,
        in_specs=placed,
        out_specs=(
            P(None, "gauss", "view"),
            P(None, "gauss", "view"),
            P(None, "gauss", "view"),
            P(),
            P(),
            P(),
            P(),
            P(),
            P(),
            P(),
        ),
        check_vma=False,
    )
```

```python
import functools
import math

import jax
import jax.numpy as jnp
from jax import lax
from jax.experimental import pallas as pl
from jax.experimental.pallas import tpu as pltpu
from jax.sharding import PartitionSpec as P

MESH = pl.DeviceIdType.MESH
ENTRY_COUNT, ATTRS, GAUSS = 20480, 59, 20480
HALF = GAUSS // 2
BLOCK, LANES = 128, 128
VIEWS, OWN = 8, 2560
CHAINS, SPREAD = 8, 4
WIDE, COLS, BONES, TABLE = 256, 512, 24, 192
PIECE, PLANE, DEPTH, HIGHS = 56, 16, 8, 4
ROWS = PIECE * PLANE


def scatter_kernel(rows_ref, ids_ref, grads_ref, out_ref, pos_ref, vals_a, vals_b, *accs):
    def zero(i, c):
        for a in accs:
            a[pl.ds(pl.multiple_of(i * 128, 128), 128), :] = jnp.zeros((128, 128), jnp.float32)
        return c

    lax.fori_loop(0, HALF // 128, zero, 0)

    def turn(off, vals):
        o = pl.multiple_of(off, 128)
        x = grads_ref[0, :, pl.ds(o, 128)].astype(jnp.float32)
        x = jnp.concatenate([x, jnp.zeros((64 - ATTRS, 128), jnp.float32)], axis=0)
        upper = ids_ref[:, pl.ds(o, 128)] >= HALF
        vals[...] = jnp.concatenate([jnp.where(upper, 0.0, x), jnp.where(upper, x, 0.0)], axis=0).T

    def add(off, vals):
        for j in range(BLOCK // CHAINS):
            r = [rows_ref[off + j * CHAINS + k] for k in range(CHAINS)]
            new = [
                accs[k][pl.ds(r[k], 1), :] + vals[j * CHAINS + k : j * CHAINS + k + 1, :]
                for k in range(CHAINS)
            ]
            for k in range(CHAINS):
                accs[k][pl.ds(r[k], 1), :] = new[k]

    turn(0, vals_a)

    def step(i, c):
        off = pl.multiple_of(i * (2 * BLOCK), 2 * BLOCK)
        turn(off + BLOCK, vals_b)
        add(off, vals_a)
        turn(jnp.minimum(off + 2 * BLOCK, ENTRY_COUNT - BLOCK), vals_a)
        add(off + BLOCK, vals_b)
        return c

    lax.fori_loop(0, ENTRY_COUNT // (2 * BLOCK), step, 0)

    def finish(i, c):
        for u in range(SPREAD):
            off = pl.multiple_of(i * (128 * SPREAD) + u * 128, 128)
            s = accs[0][pl.ds(off, 128), :]
            for a in accs[1:]:
                s = s + a[pl.ds(off, 128), :]
            t = s.T.astype(jnp.bfloat16)
            owner = off // OWN
            cols = pl.ds(pl.multiple_of(off - owner * OWN, 128), 128)
            out_ref[owner, :, cols] = t[:64]
            out_ref[owner + VIEWS // 2, :, cols] = t[64:]
            pos_ref[owner, :, cols] = t[:4]
            pos_ref[owner + VIEWS // 2, :, cols] = t[64:68]
        return c

    lax.fori_loop(0, HALF // (128 * SPREAD), finish, 0)


def scatter(grads, ids):
    vmem = pl.BlockSpec(memory_space=pltpu.VMEM)
    flat = ids.reshape(-1)
    return pl.pallas_call(
        scatter_kernel,
        out_shape=(
            jax.ShapeDtypeStruct((VIEWS, 64, OWN), jnp.bfloat16),
            jax.ShapeDtypeStruct((VIEWS, 4, OWN), jnp.bfloat16),
        ),
        in_specs=[pl.BlockSpec(memory_space=pltpu.SMEM), vmem, vmem],
        out_specs=(vmem, vmem),
        scratch_shapes=[pltpu.VMEM((BLOCK, 128), jnp.float32)] * 2
        + [pltpu.VMEM((HALF, 128), jnp.float32)] * CHAINS,
        compiler_params=pltpu.CompilerParams(vmem_limit_bytes=58 * 1024 * 1024),
        name="scatter",
    )(jnp.where(flat >= HALF, flat - HALF, flat), ids, grads)


def place():
    view, gauss = lax.axis_index("view"), lax.axis_index("gauss")
    return view // 2, lax.rem(view, 2), gauss // PLANE, lax.rem(gauss, PLANE)


def plane_peer(step):
    high, core, low, spot = place()
    return (high * 2 + core, low * PLANE + lax.rem(spot + step, PLANE))


def depth_peer(step):
    high, core, low, spot = place()
    level = lax.rem(high * 2 + low + step, DEPTH)
    return ((level // 2) * 2 + core, lax.rem(level, 2) * PLANE + spot)


def core_peer():
    high, core, low, spot = place()
    return (high * 2 + 1 - core, low * PLANE + spot)


def view_peer(step):
    return (lax.rem(lax.axis_index("view") + step, VIEWS), lax.axis_index("gauss"))


def high_peer(step):
    high, core, low, spot = place()
    return (lax.rem(high + step, HIGHS) * 2 + core, low * PLANE + spot)


def cross_peer(step):
    high, core, low, spot = place()
    return (lax.rem(high + step, HIGHS) * 2 + 1 - core, low * PLANE + spot)


def each(first, last, action):
    def one(step, carry):
        action(step)
        return carry

    lax.fori_loop(first, last, one, 0)


def greet(barrier, peer, count):
    each(
        1,
        count,
        lambda step: pl.semaphore_signal(
            barrier, inc=1, device_id=peer(step), device_id_type=MESH
        ),
    )


def remote(src, dst, sems, step, peer):
    return pltpu.make_async_remote_copy(
        src_ref=src,
        dst_ref=dst,
        send_sem=sems.at[0, step],
        recv_sem=sems.at[1, step],
        device_id=peer,
        device_id_type=MESH,
    )


def dot(left, right):
    return jnp.dot(left, right, preferred_element_type=jnp.float32)


def over_lanes(left, right):
    return lax.dot_general(
        left, right, (((1,), (1,)), ((), ())), preferred_element_type=jnp.float32
    )


def halves(value, count):
    parts = []
    for _ in range(count):
        part = value.astype(jnp.bfloat16)
        parts.append(part)
        value = value - part.astype(jnp.float32)
    return parts


def silu_pair(value):
    sig = 0.5 * jnp.tanh(0.5 * value) + 0.5
    act = value * sig
    return act.astype(jnp.bfloat16), sig + act * (1.0 - sig)


def step_kernel(
    factor,
    part,
    pos_part,
    feats,
    code_tab,
    subj,
    bone_ids,
    skin_w,
    canon,
    bone_tf,
    w_first,
    w_second,
    w_third,
    biases,
    w_head,
    attr_out,
    feat_out,
    skin_out,
    out,
    inputs,
    act_one,
    act_two,
    act_three,
    slope_one,
    slope_two,
    slope_three,
    back_one,
    back_two,
    back_three,
    hots,
    blends,
    points,
    shifts,
    turned,
    code_parts,
    bias_cols,
    head_rows,
    head_cols,
    bone_parts,
    bone_sum,
    bias_sum,
    subj_sum,
    pos_recv,
    half_recv,
    half_send,
    own_recv,
    pay,
    near,
    plane,
    depth,
    sems_pos,
    sems_half,
    sems_own,
    sems_near,
    sems_plane,
    sems_depth,
    sems_back,
):
    high, core, low, spot = place()
    view = high * 2 + core
    level = high * 2 + low
    barrier = pltpu.get_barrier_semaphore()
    greet(barrier, plane_peer, PLANE)
    greet(barrier, depth_peer, DEPTH)
    greet(barrier, cross_peer, HIGHS)
    pl.semaphore_signal(barrier, inc=1, device_id=core_peer(), device_id_type=MESH)
    pl.semaphore_wait(barrier, PLANE - 1 + DEPTH - 1 + HIGHS - 1 + 1)

    def pos_copy(step):
        return remote(
            pos_part.at[lax.rem(view + step, VIEWS)], pos_recv.at[view], sems_pos, step, view_peer(step)
        )

    def half_copy(step):
        slot = lax.rem(high + step, HIGHS)
        return remote(part.at[slot * 2 + 1 - core], half_recv.at[slot], sems_half, step, core_peer())

    def own_copy(step):
        return remote(
            half_send.at[lax.rem(high + step, HIGHS)], own_recv.at[high], sems_own, step, high_peer(step)
        )

    each(1, VIEWS, lambda step: pos_copy(step).start())
    half_order = lambda step: half_copy(step).start()
    each(1, HIGHS, half_order)
    half_order(0)
    pos_recv[view] = pos_part[view]

    turned[0] = w_first[...].T
    turned[1] = w_second[...].T
    turned[2] = w_third[...].T
    code_parts[...] = (
        jnp.concatenate([p.astype(jnp.float32) for p in halves(code_tab[...], 3)], axis=0)
        .T.astype(jnp.bfloat16)
    )
    bias_cols[...] = jnp.concatenate([biases[...], jnp.zeros((5, WIDE), jnp.float32)], axis=0).T
    head8 = jnp.concatenate(
        [w_head[...].astype(jnp.float32), jnp.zeros((5, WIDE), jnp.float32)], axis=0
    )
    head_rows[...] = head8.astype(jnp.bfloat16)
    head_cols[...] = head8.T.astype(jnp.bfloat16)
    blank = jnp.zeros((4, TABLE), jnp.float32)
    table = jnp.concatenate(
        [bone_tf[0:4], blank, bone_tf[4:8], blank, bone_tf[8:12], blank], axis=0
    )
    bone_parts[...] = jnp.concatenate(
        [p.astype(jnp.float32) for p in halves(table, 2)], axis=0
    ).astype(jnp.bfloat16)
    bone_sum[...] = jnp.zeros_like(bone_sum)
    bias_sum[...] = jnp.zeros_like(bias_sum)
    subj_sum[...] = jnp.zeros_like(subj_sum)

    def forward(chunk):
        cols = pl.ds(pl.multiple_of(chunk * COLS, COLS), COLS)
        subject = subj[:, cols]
        hot = (lax.rem(lax.broadcasted_iota(jnp.int32, (24, COLS), 0), 8) == subject).astype(
            jnp.float32
        ).astype(jnp.bfloat16)
        value = (feats[:, cols].astype(jnp.float32) + dot(code_parts[...], hot)).astype(jnp.bfloat16)
        inputs[:, cols] = value
        layers = (
            (w_first, act_one, slope_one),
            (w_second, act_two, slope_two),
            (w_third, act_three, slope_three),
        )
        for index, (weight, act, slope) in enumerate(layers):
            value, lean = silu_pair(dot(weight[...], value) + bias_cols[:, index : index + 1])
            act[:, cols] = value
            slope[:, cols] = lean
        rest = jnp.concatenate(
            [canon[0, :, cols], canon[1, :, cols], canon[2, :, cols], jnp.ones((1, COLS), jnp.float32),
             jnp.zeros((4, COLS), jnp.float32)],
            axis=0,
        )
        points[:, cols] = rest + dot(head_rows[...], value)
        index = lax.broadcasted_iota(jnp.int32, (TABLE, COLS), 0)
        for k in range(4):
            column = subject * BONES + bone_ids[k, :, cols]
            hot = (index == column).astype(jnp.float32).astype(jnp.bfloat16)
            hots[k, :, cols] = hot
            both = dot(bone_parts[...], hot)
            blends[k, :, cols] = both[:24] + both[24:]

    def own_start(step):
        half_copy(step).wait()
        slot = lax.rem(high + step, HIGHS)
        mine = part[slot * 2 + core].astype(jnp.float32)
        half_send[slot] = (mine + half_recv[slot].astype(jnp.float32)).astype(jnp.bfloat16)

    def own_send(step):
        own_start(step)
        own_copy(step).start()

    each(0, 2, forward)
    each(1, HIGHS, own_send)
    own_start(0)
    each(2, OWN // COLS, forward)
    each(1, VIEWS, lambda step: pos_copy(step).wait())

    def backward(chunk):
        cols = pl.ds(pl.multiple_of(chunk * COLS, COLS), COLS)
        pos = pos_recv[0, :, cols].astype(jnp.float32)
        for source in range(1, VIEWS):
            pos = pos + pos_recv[source, :, cols].astype(jnp.float32)
        pulls = [pos[i : i + 1] for i in range(3)]
        point = points[:, cols]
        shift = jnp.zeros((8, COLS), jnp.float32)
        for k in range(4):
            blend = blends[k, :, cols]
            moved = pulls[0] * blend[0:8] + pulls[1] * blend[8:16] + pulls[2] * blend[16:24]
            skin_out[k, :, cols] = jnp.sum(moved * point, axis=0, keepdims=True)
            weight = skin_w[k, :, cols]
            shift = shift + weight * moved
            spread = jnp.concatenate([(weight * pull) * point for pull in pulls], axis=0)
            pair = jnp.concatenate([p.astype(jnp.float32) for p in halves(spread, 2)], axis=0)
            bone_sum[...] += over_lanes(pair.astype(jnp.bfloat16), hots[k, :, cols])
        shift = shift.astype(jnp.bfloat16)
        shifts[:, cols] = shift
        value = (dot(head_cols[...], shift) * slope_three[:, cols]).astype(jnp.bfloat16)
        back_three[:, cols] = value
        tally(2, value)
        value = (dot(turned[2], value) * slope_two[:, cols]).astype(jnp.bfloat16)
        back_two[:, cols] = value
        tally(1, value)
        value = (dot(turned[1], value) * slope_one[:, cols]).astype(jnp.bfloat16)
        back_one[:, cols] = value
        hot = (lax.broadcasted_iota(jnp.int32, (8, COLS), 0) == subj[:, cols]).astype(
            jnp.float32
        ).astype(jnp.bfloat16)
        subj_sum[...] += over_lanes(hot, value)
        feat_out[:, cols] = dot(turned[0], value).astype(jnp.bfloat16)

    def tally(index, value):
        wide = value.astype(jnp.float32)
        total = bias_sum[index - 1]
        for lane in range(COLS // LANES):
            total = total + wide[:, lane * LANES : (lane + 1) * LANES]
        bias_sum[index - 1] = total

    each(0, OWN // COLS, backward)

    def store(row, value):
        count = value.shape[0]
        pay[0, row : row + count, :] = value[:, :LANES]
        pay[1, row : row + count, :] = value[:, LANES:]

    store(512, over_lanes(back_three[...], act_two[...]))
    store(256, over_lanes(back_two[...], act_one[...]))
    store(0, over_lanes(back_one[...], inputs[...]))
    store(768, over_lanes(shifts[...], act_three[...]))
    groups = subj_sum[...]
    store(
        776,
        jnp.concatenate(
            [jnp.sum(groups, axis=0, keepdims=True)]
            + [jnp.sum(bias_sum[index].T, axis=0, keepdims=True) for index in range(2)]
            + [jnp.zeros((5, WIDE), jnp.float32)],
            axis=0,
        ),
    )
    code = dot(
        jnp.concatenate([p.astype(jnp.float32) for p in halves(groups, 3)], axis=0).astype(jnp.bfloat16),
        w_first[...],
    )
    store(784, code[0:8] + code[8:16] + code[16:24])
    bone = bone_sum[0:24] + bone_sum[24:48]
    store(792, jnp.concatenate([bone, jnp.zeros((24, WIDE - TABLE), jnp.float32)], axis=1))
    store(816, jnp.zeros((ROWS - 816, WIDE), jnp.float32))

    def finish_attrs():
        each(1, HIGHS, lambda step: own_copy(step).wait())
        own_recv[high] = half_send[high]

        def piece(index):
            cols = pl.ds(pl.multiple_of(index * 256, 256), 256)
            total = own_recv[0, :, cols].astype(jnp.float32)
            for source in range(1, HIGHS):
                total = total + own_recv[source, :, cols].astype(jnp.float32)
            for row in range(ATTRS):
                attr_out[row, :, cols] = total[row : row + 1]

        each(0, OWN // 256, piece)

    reduce_all(
        factor, finish_attrs, pay, out, near, plane, depth, sems_near, sems_plane, sems_depth, sems_back
    )


def reduce_all(
    factor, cover, pay, out, near, plane, depth, sems_near, sems_plane, sems_depth, sems_back
):
    high, core, low, spot = place()
    level = high * 2 + low
    swap = remote(pay.at[1 - core], near, sems_near, 0, core_peer())
    swap.start()
    swap.wait()
    near[...] = near[...] + pay[core]

    def piece(index):
        return pl.ds(pl.multiple_of(index * PIECE, PIECE), PIECE)

    def plane_copy(step):
        return remote(
            near.at[piece(lax.rem(spot + step, PLANE))],
            plane.at[spot],
            sems_plane,
            step,
            plane_peer(step),
        )

    each(1, PLANE, lambda step: plane_copy(step).start())
    plane[spot] = near[piece(spot)]
    each(1, PLANE, lambda step: plane_copy(step).wait())
    total = plane[0]
    for index in range(1, PLANE):
        total = total + plane[index]
    depth[level] = total

    def depth_copy(step):
        return remote(depth.at[level], depth.at[level], sems_depth, step, depth_peer(step))

    each(1, DEPTH, lambda step: depth_copy(step).start())
    each(1, DEPTH, lambda step: depth_copy(step).wait())
    total = depth[0]
    for index in range(1, DEPTH):
        total = total + depth[index]
    out[core, piece(spot)] = total * factor

    def back_copy(step):
        return remote(
            out.at[core, piece(spot)], out.at[core, piece(spot)], sems_back, step, plane_peer(step)
        )

    each(1, PLANE, lambda step: back_copy(step).start())
    cover()
    each(1, PLANE, lambda step: back_copy(step).wait())
    last = remote(out.at[core], out.at[core], sems_near, 1, core_peer())
    last.start()
    last.wait()


def unpack_kernel(attrs, feats, skins, sums, attr_out, feat_out, skin_out, first, second, third, bias, head, code, bone):
    attr_out[...] = attrs[...]
    feat_out[...] = feats[...]
    skin_out[...] = skins[...]
    for half in range(2):
        lanes = slice(half * LANES, (half + 1) * LANES)
        first[:, lanes] = sums[half, 0:256]
        second[:, lanes] = sums[half, 256:512]
        third[:, lanes] = sums[half, 512:768]
        head[:, lanes] = sums[half, 768:771]
        bias[:, lanes] = sums[half, 776:779]
        code[:, lanes] = sums[half, 784:792]
        lanes = slice(half * LANES, min((half + 1) * LANES, TABLE))
        for i in range(3):
            start = 792 + 8 * i
            bone[4 * i : 4 * i + 4, lanes] = sums[half, start : start + 4, : lanes.stop - lanes.start]


def body(
    entry_grads,
    vis_ids,
    feats,
    code_tab,
    subj_ids,
    bone_ids,
    skin_w,
    canon_pos,
    bone_tf,
    w_first,
    w_second,
    w_third,
    biases,
    w_head,
):
    factor = 1.0 / math.sqrt(GAUSS * lax.axis_size("gauss"))
    part, pos_part = scatter(entry_grads, vis_ids)
    vmem = pl.BlockSpec(memory_space=pltpu.VMEM)
    f32, b16 = jnp.float32, jnp.bfloat16
    shape = jax.ShapeDtypeStruct
    sems = lambda count: pltpu.SemaphoreType.DMA((2, count))
    results = (
        shape((ATTRS, 1, OWN), f32),
        shape((WIDE, OWN), b16),
        shape((4, 1, OWN), f32),
    )
    values = pl.pallas_call(
        functools.partial(step_kernel, factor),
        out_shape=results + (shape((2, ROWS, LANES), f32),),
        in_specs=[vmem] * 14,
        out_specs=(vmem,) * 4,
        scratch_shapes=[pltpu.VMEM((WIDE, OWN), b16)] * 4
        + [pltpu.VMEM((WIDE, OWN), f32)] * 3
        + [pltpu.VMEM((WIDE, OWN), b16)] * 3
        + [
            pltpu.VMEM((4, TABLE, OWN), b16),
            pltpu.VMEM((4, 24, OWN), f32),
            pltpu.VMEM((8, OWN), f32),
            pltpu.VMEM((8, OWN), b16),
            pltpu.VMEM((3, WIDE, WIDE), b16),
            pltpu.VMEM((WIDE, 24), b16),
            pltpu.VMEM((WIDE, 8), f32),
            pltpu.VMEM((8, WIDE), b16),
            pltpu.VMEM((WIDE, 8), b16),
            pltpu.VMEM((48, TABLE), b16),
            pltpu.VMEM((48, TABLE), f32),
            pltpu.VMEM((2, WIDE, LANES), f32),
            pltpu.VMEM((8, WIDE), f32),
            pltpu.VMEM((VIEWS, 4, OWN), b16),
            pltpu.VMEM((HIGHS, 64, OWN), b16),
            pltpu.VMEM((HIGHS, 64, OWN), b16),
            pltpu.VMEM((HIGHS, 64, OWN), b16),
            pltpu.VMEM((2, ROWS, LANES), f32),
            pltpu.VMEM((ROWS, LANES), f32),
            pltpu.VMEM((PLANE, PIECE, LANES), f32),
            pltpu.VMEM((DEPTH, PIECE, LANES), f32),
            sems(VIEWS),
            sems(HIGHS),
            sems(HIGHS),
            sems(2),
            sems(PLANE),
            sems(DEPTH),
            sems(PLANE),
        ],
        compiler_params=pltpu.CompilerParams(
            collective_id=0, has_side_effects=True, vmem_limit_bytes=50 * 1024 * 1024
        ),
        name="step",
    )(
        part,
        pos_part,
        feats[:, 0],
        code_tab.T,
        subj_ids,
        bone_ids,
        skin_w,
        canon_pos,
        bone_tf,
        w_first,
        w_second,
        w_third,
        biases,
        w_head,
    )
    attrs, feat, skins, first, second, third, bias_rows, head, code, bone = pl.pallas_call(
        unpack_kernel,
        out_shape=results
        + (shape((WIDE, WIDE), f32),) * 3
        + (shape((3, WIDE), f32), shape((3, WIDE), f32), shape((8, WIDE), f32), shape((12, TABLE), f32)),
        in_specs=[vmem] * 4,
        out_specs=(vmem,) * 10,
        compiler_params=pltpu.CompilerParams(vmem_limit_bytes=16 * 1024 * 1024),
        name="unpack",
    )(*values)
    return (
        attrs,
        feat[:, None, :],
        skins,
        first,
        second,
        third,
        bias_rows,
        head,
        code.T,
        bone,
    )


def solution(mesh):
    placed = (
        P("view", None, "gauss"),
        P("view", "gauss"),
        P(None, "gauss", "view"),
        P(),
        P("gauss", "view"),
        P(None, "gauss", "view"),
        P(None, "gauss", "view"),
        P(None, "gauss", "view"),
        P(),
        P(),
        P(),
        P(),
        P(),
        P(),
    )
    return jax.shard_map(
        body,
        mesh=mesh,
        in_specs=placed,
        out_specs=(
            P(None, "gauss", "view"),
            P(None, "gauss", "view"),
            P(None, "gauss", "view"),
            P(),
            P(),
            P(),
            P(),
            P(),
            P(),
            P(),
        ),
        check_vma=False,
    )
```
